32 devices in a mesh: dp: 8 (over z, y), tensor: 4 (over x, core).
Axes of the slice: x: 2, y: 2, z: 4, core: 2. Of those that a mesh axis runs over, the one named last changes fastest.
Arguments:
- tokens: bfloat16 [16, 1024, 768], P('dp', 'tensor'), may hold values from -6 to 6
- segment_ids: int32 [16, 1024], P('dp'), may hold values from 0 to 11, never falling along the last dimension, each value on 1 to 384 neighbouring positions
- entry_weight: bfloat16 [768, 3, 768], P('dp', None, 'tensor'), may hold values from -0.21875 to 0.21875
- entry_bias: bfloat16 [2, 768], P(None, ('tensor', 'dp')), may hold values from -4 to 4
- mixing_weight: bfloat16 [768, 768], P('tensor', 'dp'), may hold values from -1.25 to 1.25
- mixing_bias: float32 [768], P(('dp', 'tensor')), may hold values from -4 to 4
- first_gain: float32 [768], P(('dp', 'tensor')), may hold values from 0.5 to 1.5
- first_shift: float32 [768], P(('dp', 'tensor')), may hold values from -4 to 4
- expand_weight: bfloat16 [768, 3072], P('dp', 'tensor'), may hold values from -0.21875 to 0.21875
- expand_bias: bfloat16 [3072], P(('tensor', 'dp')), may hold values from -4 to 4
- narrowing_matrix: bfloat16 [3072, 768], P('tensor', 'dp'), may hold values from -0.15625 to 0.15625
- reduce_bias: float32 [768], P(('dp', 'tensor')), may hold values from -4 to 4
- second_gain: float32 [768], P(('dp', 'tensor')), may hold values from 0.5 to 1.5
- second_shift: float32 [768], P(('dp', 'tensor')), may hold values from -4 to 4
- layer_cotangent: bfloat16 [16, 1024, 768], P('dp', 'tensor'), may hold values from -6 to 6
Outputs:
- layer_output: bfloat16 [16, 1024, 768], P('dp', 'tensor')
- tokens_gradient: float32 [16, 1024, 768], P('dp', 'tensor')
- entry_weight_gradient: float32 [768, 3, 768], P('dp', None, 'tensor')
- entry_bias_gradient: float32 [2, 768], P(None, ('tensor', 'dp'))
- mixing_weight_gradient: float32 [768, 768], P('tensor', 'dp')
- mixing_bias_gradient: float32 [768], P(('dp', 'tensor'))
- first_gain_gradient: float32 [768], P(('dp', 'tensor'))
- first_shift_gradient: float32 [768], P(('dp', 'tensor'))
- expand_weight_gradient: float32 [768, 3072], P('dp', 'tensor')
- expand_bias_gradient: float32 [3072], P(('tensor', 'dp'))
- reduce_weight_gradient: float32 [3072, 768], P('tensor', 'dp')
- reduce_bias_gradient: float32 [768], P(('dp', 'tensor'))
- second_gain_gradient: float32 [768], P(('dp', 'tensor'))
- second_shift_gradient: float32 [768], P(('dp', 'tensor'))
The draws below stay inside these ranges and needn't reach their ends.
Inputs may be any that keep to these rules, and one draw needn't show every extreme that they name: `segment_ids`: within each packed sequence the ids never fall and every id from 0 to 11 occurs; a document has 1 to 384 tokens, and one has exactly 384.
All inputs are finite; a program needn't handle non-finite values.
Results may differ from the reference program's by a relative error of at most 0.018.
Values may be sent and summed in bfloat16 or wider, within the bound.
No kernel may reach another device: no remote copies, remote signals or barrier semaphores. Data moves between devices by JAX's collectives and lax.ppermute only.
A program may use at most 128 MiB of HBM per device.

```python
import math
import jax
import jax.numpy as jnp
import numpy as np
from jax import lax

D = 768
HEADS = 12
HEAD = 64
FF = 3072
LEN = 1024
DOCS = 12
DOC_MOST = 384
SEQS = 16


def block_scale(rng, dims, pieces, least, top_value):
    factor_of = 1.0
    for axis_at, blocks in pieces:
        draws = jax.random.uniform(jax.random.fold_in(jax.random.fold_in(rng, 6), axis_at), (blocks,), jnp.float32, least / len(pieces), top_value / len(pieces))
        factor_of = factor_of * jnp.repeat(jnp.exp(draws), dims[axis_at] // blocks).reshape((-1,) + (1,) * (len(dims) - 1 - axis_at))
    return factor_of


def split_up(count, total, limit, lean):
    portions = [(1 << 20) // math.isqrt(rank ** lean) + 1 for rank in range(2, count + 1)]
    surplus, holding = total - limit - (count - 1), [1] * (count - 1)
    while surplus > 0:
        movable = [i for i in range(count - 1) if holding[i] < limit]
        whole, left = sum([portions[i] for i in movable]), surplus
        for i in movable:
            more = min(limit - holding[i], max(1, left * portions[i] // whole), surplus)
            holding[i] = holding[i] + more
            surplus = surplus - more
    return np.array([limit] + holding)


def ragged(stream_key, count, total, most, slope):
    if count == 2:
        one = jax.random.randint(stream_key, (), max(1, total - most), min(most, total - 1) + 1)
        return jnp.stack([one, total - one])
    sizes = jnp.asarray(split_up(count, total, most, slope), jnp.int32)
    pairs = (count - 1) // 2
    source_of, taker = sizes[1:1 + 2 * pairs:2], sizes[2:2 + 2 * pairs:2]
    room = jnp.minimum(source_of - 1, most - taker)
    moved = jax.random.randint(jax.random.fold_in(stream_key, 1), (pairs,), 0, 1 << 20) % (room + 1)
    sizes = sizes.at[1:1 + 2 * pairs:2].set(source_of - moved).at[2:2 + 2 * pairs:2].set(taker + moved)
    return sizes[jax.random.permutation(jax.random.fold_in(stream_key, 2), count)]


def bell_draw(key, extent, deviation, limit, cuts=(), kind=jnp.bfloat16):
    drawn = deviation * jax.random.normal(key, extent, jnp.float32)
    if cuts:
        drawn = drawn * block_scale(key, extent, cuts, -0.22, 0.18)
    return jnp.clip(drawn, -limit, limit).astype(kind)


def setup_inputs(seed: int = 0) -> dict:
    key_list = jax.random.split(jax.random.key(seed), 16)
    tokens = bell_draw(key_list[0], (SEQS, LEN, D), 1.0, 6.0, ((0, 8), (1, 4)))
    segment_ids = jax.vmap(lambda own: jnp.searchsorted(jnp.cumsum(ragged(own, DOCS, LEN, DOC_MOST, 2)), jnp.arange(LEN), side="right"))(jax.random.split(key_list[1], SEQS)).reshape((SEQS, LEN)).astype(jnp.int32)
    entry_weight = bell_draw(key_list[2], (D, 3, D), D ** -0.5, 0.21875, ((0, 8), (2, 4)))
    entry_bias = bell_draw(key_list[3], (2, D), 0.3, 4.0, ((1, 32),))
    mixing_weight = bell_draw(key_list[4], (D, D), (D // 32) ** -0.5, 1.25, ((0, 4), (1, 8)))
    mixing_bias = bell_draw(key_list[5], (D,), 0.3, 4.0, ((0, 32),), jnp.float32)
    first_gain = jnp.clip(1.0 + 0.1 * jax.random.normal(key_list[6], (D,), jnp.float32), 0.5, 1.5)
    first_shift = bell_draw(key_list[7], (D,), 0.3, 4.0, ((0, 32),), jnp.float32)
    expand_weight = bell_draw(key_list[8], (D, FF), D ** -0.5, 0.21875, ((0, 8), (1, 4)))
    expand_bias = bell_draw(key_list[9], (FF,), 0.3, 4.0, ((0, 32),))
    narrowing_matrix = bell_draw(key_list[10], (FF, D), (FF // 2) ** -0.5, 0.15625, ((0, 4), (1, 8)))
    reduce_bias = bell_draw(key_list[11], (D,), 0.3, 4.0, ((0, 32),), jnp.float32)
    second_gain = jnp.clip(1.0 + 0.1 * jax.random.normal(key_list[12], (D,), jnp.float32), 0.5, 1.5)
    second_shift = bell_draw(key_list[13], (D,), 0.3, 4.0, ((0, 32),), jnp.float32)
    layer_cotangent = bell_draw(key_list[14], (SEQS, LEN, D), 1.0, 6.0, ((0, 8), (1, 4)))
    return {"tokens": tokens, "segment_ids": segment_ids, "entry_weight": entry_weight, "entry_bias": entry_bias, "mixing_weight": mixing_weight, "mixing_bias": mixing_bias, "first_gain": first_gain, "first_shift": first_shift, "expand_weight": expand_weight, "expand_bias": expand_bias, "narrowing_matrix": narrowing_matrix, "reduce_bias": reduce_bias, "second_gain": second_gain, "second_shift": second_shift, "layer_cotangent": layer_cotangent}


highest = lax.Precision.HIGHEST

@jax.custom_vjp
def low(v):
    return lax.optimization_barrier(v.astype(jnp.bfloat16)).astype(jnp.float32)

@jax.custom_vjp
def low_back(v):
    return v

def low_keep(v):
    return (low(v), None)

def low_pass(kept, grad):
    return (grad,)

def back_keep(v):
    return (v, None)

def back_low(kept, grad):
    return (low(grad),)
low.defvjp(low_keep, low_pass)
low_back.defvjp(back_keep, back_low)

def layer_norm(values, gain_row, shift_row):
    center = values - lax.optimization_barrier(jnp.mean(values, axis=-1, keepdims=True))
    spread = lax.optimization_barrier(jnp.mean(center * center, axis=-1, keepdims=True))
    return center * lax.rsqrt(spread + 1e-12) * gain_row + shift_row

def gelu_exact(values):
    return 0.5 * values * (1.0 + jax.scipy.special.erf(values * 0.7071067811865476))

def attend_one(packed):
    queries, key_rows, values, segments = packed
    scores = jnp.einsum('qhe,khe->hqk', queries, key_rows, precision=highest) * HEAD ** (-0.5)
    scores = low_back(scores)
    matching_passage_mask = segments[:, None] == segments[None, :]
    scores = jnp.where(matching_passage_mask[None, :, :], scores, -1e+30)
    attention_probability_matrix = low(jax.nn.softmax(scores, axis=-1))
    return jnp.einsum('hqk,khe->qhe', attention_probability_matrix, values, precision=highest)

def layer_forward(params, tokens, segments):
    entry_weight, entry_bias, mixing_weight, mixing_bias, first_gain, first_shift, expand_weight, expand_bias, narrowing_matrix, reduce_bias, second_gain, second_shift = params
    batch_size, length, features = tokens.shape
    full_bias = jnp.stack([entry_bias[0], jnp.zeros_like(entry_bias[0]), entry_bias[1]])
    projected = jnp.einsum('bld,dcn->blcn', tokens, entry_weight, precision=highest) + full_bias
    projected = low(low_back(projected))
    head_shape = (batch_size, length, HEADS, HEAD)
    queries = projected[:, :, 0].reshape(head_shape)
    key_rows = projected[:, :, 1].reshape(head_shape)
    values = projected[:, :, 2].reshape(head_shape)
    context = lax.map(jax.checkpoint(attend_one), (queries, key_rows, values, segments))
    context = low(low_back(context.reshape(batch_size, length, features)))
    attended = low_back(jnp.einsum('bln,nd->bld', context, mixing_weight, precision=highest))
    first_sum = tokens + attended + mixing_bias
    normed = layer_norm(first_sum, first_gain, first_shift)
    standardized_bfloat_copy = low(normed)
    inner = low_back(jnp.einsum('bld,df->blf', standardized_bfloat_copy, expand_weight, precision=highest) + expand_bias)
    gelu_activations = low(gelu_exact(inner))
    branch = low_back(jnp.einsum('blf,fd->bld', gelu_activations, narrowing_matrix, precision=highest))
    second_sum = normed + branch + reduce_bias
    return layer_norm(second_sum, second_gain, second_shift)

def add_pair(left, right):
    return left + right

def reference(tokens, segment_ids, entry_weight, entry_bias, mixing_weight, mixing_bias, first_gain, first_shift, expand_weight, expand_bias, narrowing_matrix, reduce_bias, second_gain, second_shift, layer_cotangent):
    params = (entry_weight.astype(jnp.float32), entry_bias.astype(jnp.float32), mixing_weight.astype(jnp.float32), mixing_bias.astype(jnp.float32), first_gain.astype(jnp.float32), first_shift.astype(jnp.float32), expand_weight.astype(jnp.float32), expand_bias.astype(jnp.float32), narrowing_matrix.astype(jnp.float32), reduce_bias.astype(jnp.float32), second_gain.astype(jnp.float32), second_shift.astype(jnp.float32))
    group_size = math.gcd(SEQS, max(1, 4096 // LEN))
    step_count = SEQS // group_size
    token_blocks = tokens.astype(jnp.float32).reshape(step_count, group_size, LEN, D)
    segment_blocks = segment_ids.reshape(step_count, group_size, LEN)
    cotangent_blocks = layer_cotangent.astype(jnp.float32).reshape(step_count, group_size, LEN, D)

    def one_block(totals, packed):
        token_block, segment_block, cotangent_block = packed

        def forward(trainable_tensor_sequence, token_input):
            return layer_forward(trainable_tensor_sequence, token_input, segment_block)
        output, pullback = jax.vjp(forward, params, token_block)
        param_grads, token_grads = pullback(cotangent_block)
        totals = jax.tree.map(add_pair, totals, param_grads)
        return (totals, (output.astype(jnp.bfloat16), token_grads))
    zero_grads = jax.tree.map(jnp.zeros_like, params)
    totals, (outputs, token_grads) = lax.scan(one_block, zero_grads, (token_blocks, segment_blocks, cotangent_blocks))
    layer_output = outputs.reshape(SEQS, LEN, D)
    tokens_gradient = token_grads.reshape(SEQS, LEN, D)
    return (layer_output, tokens_gradient, totals[0], totals[1], totals[2], totals[3], totals[4], totals[5], totals[6], totals[7], totals[8], totals[9], totals[10], totals[11])
```

```python
import functools

import jax
import jax.numpy as jnp
from jax import lax
from jax.sharding import PartitionSpec as P

HEAD = 64
BF = jnp.bfloat16
F32 = jnp.float32
AXES = ("dp", "tensor")


def dot(a, b, ca, cb):
    return lax.dot_general(a, b, (((ca,), (cb,)), ((), ())), preferred_element_type=F32)


def norm_forward(values, gain, shift):
    center = values - jnp.mean(values, axis=-1, keepdims=True)
    spread = jnp.mean(center * center, axis=-1, keepdims=True)
    scale = lax.rsqrt(spread + 1e-12)
    hat = center * scale
    return hat * gain + shift, hat, scale


def norm_backward(grad, hat, scale, gain):
    e = grad * gain
    return scale * (
        e
        - jnp.mean(e, axis=-1, keepdims=True)
        - hat * jnp.mean(e * hat, axis=-1, keepdims=True)
    )


def attend_forward(q, k, v, seg):
    rows, width = q.shape
    heads = width // HEAD
    q, k, v = (a.reshape(rows, heads, HEAD) for a in (q, k, v))
    scores = jnp.einsum("qhe,khe->hqk", q, k, preferred_element_type=F32) * HEAD**-0.5
    mask = seg[:, None] == seg[None, :]
    scores = jnp.where(mask[None], scores, -1e30)
    top = jnp.max(scores, axis=-1, keepdims=True)
    expo = jnp.exp(scores - top)
    total = jnp.sum(expo, axis=-1, keepdims=True)
    prob = (expo / total).astype(BF)
    context = jnp.einsum("hqk,khe->qhe", prob, v, preferred_element_type=F32)
    return context.astype(BF).reshape(rows, width), (top + jnp.log(total))[:, :, 0]


def attend_backward(q, k, v, seg, logs, grad):
    rows, width = q.shape
    heads = width // HEAD
    q, k, v, grad = (a.reshape(rows, heads, HEAD) for a in (q, k, v, grad))
    scores = jnp.einsum("qhe,khe->hqk", q, k, preferred_element_type=F32) * HEAD**-0.5
    mask = seg[:, None] == seg[None, :]
    scores = jnp.where(mask[None], scores, -1e30)
    prob = jnp.exp(scores - logs[:, :, None])
    gp = jnp.einsum("qhe,khe->hqk", grad, v, preferred_element_type=F32)
    inner = jnp.sum(prob * gp, axis=-1, keepdims=True)
    gs = (prob * (gp - inner)).astype(BF)
    gq = jnp.einsum("hqk,khe->qhe", gs, k, preferred_element_type=F32) * HEAD**-0.5
    gk = jnp.einsum("hqk,qhe->khe", gs, q, preferred_element_type=F32) * HEAD**-0.5
    gv = jnp.einsum("hqk,qhe->khe", prob.astype(BF), grad, preferred_element_type=F32)
    return [a.reshape(rows, width).astype(BF) for a in (gq, gk, gv)]


def gelu_parts(inner):
    cdf = 0.5 * (1.0 + lax.erf(inner * 0.7071067811865476))
    act = inner * cdf
    slope = cdf + inner * jnp.exp(-0.5 * inner * inner) * 0.3989422804014327
    return act, slope


def local(
    dp_size,
    tensor_size,
    tokens,
    segment_ids,
    entry_weight,
    entry_bias,
    mixing_weight,
    mixing_bias,
    first_gain,
    first_shift,
    expand_weight,
    expand_bias,
    narrowing_matrix,
    reduce_bias,
    second_gain,
    second_shift,
    layer_cotangent,
):
    N, T = dp_size, tensor_size
    d = lax.axis_index("dp")
    t = lax.axis_index("tensor")
    h = t // 2
    c = t % 2

    def swap(a, dp_bit, t_bit):
        pairs = [
            (i * T + j, (i ^ dp_bit) * T + (j ^ t_bit)) for i in range(N) for j in range(T)
        ]
        return lax.ppermute(a, AXES, pairs)

    swap_h = lambda a: swap(a, 0, 2)
    swap_c = lambda a: swap(a, 0, 1)
    high_bits = []
    bit = N // 2
    while bit >= 2:
        high_bits.append(bit)
        bit //= 2

    def bit_of(b):
        return (d // b) % 2

    def put(own, got, b, axis):
        on = bit_of(b) == 1
        return jnp.stack([jnp.where(on, got, own), jnp.where(on, own, got)], axis=axis)

    def gather_step(a, b):
        blocks, rows, lanes = a.shape
        return put(a, swap(a, b, 0), b, 1).reshape(2 * blocks, rows, lanes)

    def gather_high(a):
        a = a[None]
        for b in high_bits:
            a = gather_step(a, b)
        return a

    def flat(a):
        return a.reshape(-1, a.shape[-1])

    def gather_yx(a):
        a = gather_step(a, 1)
        return flat(a), flat(swap_h(a))

    def gather_xy(a):
        other = swap_h(a)
        return flat(gather_step(a, 1)), flat(gather_step(other, 1))

    def gather_xy_one(a):
        both = jnp.concatenate([a, swap_h(a)], axis=2)
        both = gather_step(both, 1)
        lanes = a.shape[2]
        return flat(both[:, :, :lanes]), flat(both[:, :, lanes:])

    D = tokens.shape[-1]
    sl = first_gain.shape[0]
    eb = expand_bias.shape[0]
    bb = entry_bias.shape[1]
    small = jnp.concatenate(
        [
            mixing_bias,
            first_gain,
            first_shift,
            reduce_bias,
            second_gain,
            second_shift,
            entry_bias.astype(F32).reshape(-1),
            expand_bias.astype(F32),
        ]
    )
    length = small.shape[0]
    small = jnp.pad(small, (0, -length % 128)).reshape(1, 1, -1)
    small = put_t(small, swap_c(small), c)
    small = put_t(small, swap_h(small), h)
    for b in high_bits + [1]:
        small = gather_step(small, b)

    def to_chip(a):
        keep = jnp.where(h == 0, a[0], a[1])
        send = jnp.where(h == 0, a[1], a[0])
        return jnp.concatenate([keep, swap_h(send)], axis=0)

    x_own = to_chip(tokens)

    entry_flat = entry_weight.reshape(entry_weight.shape[0], -1)
    entry = gather_high(entry_flat)
    half = entry.shape[2] // 256 * 128
    entry_a = gather_yx(entry[:, :, :half])
    entry_b = gather_xy_one(entry[:, :, half:])
    entry_w = [jnp.concatenate([a, b], axis=1) for a, b in zip(entry_a, entry_b)]

    x_full = jnp.concatenate([x_own, swap_c(x_own)], axis=0)
    cot = to_chip(layer_cotangent)

    ffn = jnp.concatenate(
        [mixing_weight.T, expand_weight, narrowing_matrix.T], axis=1
    )
    ffn = gather_high(ffn)
    mw = mixing_weight.shape[0]
    ew = expand_weight.shape[1]
    cut = mw + ew
    fa = gather_yx(ffn[:, :, :cut])
    nar_w = gather_xy_one(ffn[:, :, cut:])
    mix_w = [a[:, :mw] for a in fa]
    exp_w = [a[:, mw:] for a in fa]

    six = small[:, :, : 6 * sl].reshape(N, T, 6, sl).transpose(2, 0, 1, 3).reshape(6, D)
    (mix_b, g1, s1, red_b, g2, s2) = (six[i : i + 1] for i in range(6))

    def at_t(index):
        return lax.dynamic_index_in_dim(small, index, axis=1, keepdims=False)

    mine = [at_t(t), at_t(t ^ 2)]
    ent_b = []
    exp_b = []
    for m in mine:
        e = m[:, 6 * sl : 6 * sl + 2 * bb].reshape(N, 2, bb)
        ent_b.append(e.transpose(1, 0, 2).reshape(2, -1))
        exp_b.append(m[:, 6 * sl + 2 * bb : 6 * sl + 2 * bb + eb].reshape(1, -1))

    seg = jnp.where(h == 0, segment_ids[0], segment_ids[1])
    seg = seg.reshape(2, 2, -1)
    seg = jnp.where(h == 0, seg, seg[::-1])
    seg = jnp.where(c == 0, seg, seg[:, ::-1])
    seg = seg.transpose(1, 0, 2).reshape(-1)
    half_rows = x_own.shape[0]

    def sum_cores(partial):
        return partial[:half_rows] + swap_c(partial[half_rows:].astype(BF)).astype(F32)

    q, k, v, ctx, logs = [], [], [], [], []
    mixed = 0.0
    for g in range(2):
        proj = dot(x_full, entry_w[g], 1, 0)
        width = proj.shape[1] // 3
        bias = jnp.concatenate(
            [ent_b[g][0], jnp.zeros((width,), F32), ent_b[g][1]]
        )
        proj = (proj + bias).astype(BF)
        q.append(proj[:, :width])
        k.append(proj[:, width : 2 * width])
        v.append(proj[:, 2 * width :])
        a, b = attend_forward(q[g], k[g], v[g], seg)
        ctx.append(a)
        logs.append(b)
        mixed = mixed + dot(ctx[g], mix_w[g], 1, 1)
    first_sum = x_own.astype(F32) + sum_cores(mixed) + mix_b
    normed, hat1, scale1 = norm_forward(first_sum, g1, s1)
    n_own = normed.astype(BF)
    n_full = jnp.concatenate([n_own, swap_c(n_own)], axis=0)

    act, slope = [], []
    branch = 0.0
    for g in range(2):
        inner = dot(n_full, exp_w[g], 1, 0) + exp_b[g]
        a, s = gelu_parts(inner)
        act.append(a.astype(BF))
        slope.append(s)
        branch = branch + dot(act[g], nar_w[g], 1, 1)
    second_sum = normed + sum_cores(branch) + red_b
    out, hat2, scale2 = norm_forward(second_sum, g2, s2)
    out = out.astype(BF)
    rows = tokens.shape[1]
    out_got = swap_h(out[rows:])
    layer_output = jnp.stack(
        [jnp.where(h == 0, out[:rows], out_got), jnp.where(h == 0, out_got, out[:rows])]
    )

    cot32 = cot.astype(F32)
    grad2 = norm_backward(cot32, hat2, scale2, g2)
    vec = [
        jnp.sum(cot32 * hat2, axis=0),
        jnp.sum(cot32, axis=0),
        jnp.sum(grad2, axis=0),
    ]
    gs_own = grad2.astype(BF)
    gs_full = jnp.concatenate([gs_own, swap_c(gs_own)], axis=0)

    def scatter(own, other, first):
        shape = (N, D // N, own.shape[1])
        own = own.astype(BF).reshape(shape)
        other = other.astype(BF).reshape(shape)

        def add(a, b, low=True):
            s = a.astype(F32) + b.astype(F32)
            return s.astype(BF) if low else s

        def split(a, b):
            n, r, l = a.shape
            a = a.reshape(n // 2, 2, r, l)
            on = bit_of(b) == 1
            keep = jnp.where(on, a[:, 1], a[:, 0])
            send = jnp.where(on, a[:, 0], a[:, 1])
            return keep, send

        if first == "x":
            a = add(own, swap_h(other))
            keep, send = split(a, 1)
            a = add(keep, swap(send, 1, 0))
        else:
            both = jnp.concatenate([own, other], axis=2)
            keep, send = split(both, 1)
            a = add(keep, swap(send, 1, 0))
            lanes = own.shape[2]
            a = add(a[:, :, :lanes], swap_h(a[:, :, lanes:]))
        low_first = high_bits[::-1]
        for i, b in enumerate(low_first):
            keep, send = split(a, b)
            a = add(keep, swap(send, b, 0), i + 1 < len(low_first))
        return a.reshape(D // N, -1).astype(F32)

    grad_n = 0.0
    nar_g, exp_g, exp_bg = [], [], []
    for g in range(2):
        nar_g.append(dot(gs_full, act[g], 0, 0))
        gi = (dot(gs_full, nar_w[g], 1, 0) * slope[g]).astype(BF)
        exp_bg.append(jnp.sum(gi.astype(F32), axis=0))
        exp_g.append(dot(n_full, gi, 0, 0))
        grad_n = grad_n + dot(gi, exp_w[g], 1, 1)
    nar_grad = scatter(nar_g[0], nar_g[1], "x").T
    exp_grad = scatter(exp_g[0], exp_g[1], "y")
    grad_normed = grad2 + sum_cores(grad_n)
    grad1 = norm_backward(grad_normed, hat1, scale1, g1)
    vec += [
        jnp.sum(grad_normed * hat1, axis=0),
        jnp.sum(grad_normed, axis=0),
        jnp.sum(grad1, axis=0),
    ]
    gf_own = grad1.astype(BF)
    gf_full = jnp.concatenate([gf_own, swap_c(gf_own)], axis=0)
    grad_x = 0.0
    mix_g, ent_g, ent_bg = [], [], []
    for g in range(2):
        mix_g.append(dot(gf_full, ctx[g], 0, 0))
        gc = dot(gf_full, mix_w[g], 1, 0).astype(BF)
        gq, gk, gv = attend_backward(q[g], k[g], v[g], seg, logs[g], gc)
        gp = jnp.concatenate([gq, gk, gv], axis=1)
        ent_bg.append(
            jnp.stack([jnp.sum(gq.astype(F32), axis=0), jnp.sum(gv.astype(F32), axis=0)])
        )
        ent_g.append(dot(x_full, gp, 0, 0))
        grad_x = grad_x + dot(gp, entry_w[g], 1, 1)
    mix_grad = scatter(mix_g[0], mix_g[1], "y").T
    ent_grad = scatter(ent_g[0], ent_g[1], "x")

    dx = grad1 + sum_cores(grad_x)
    dx_got = swap_h(dx[rows:].astype(BF)).astype(F32)
    tokens_gradient = jnp.stack(
        [jnp.where(h == 0, dx[:rows], dx_got), jnp.where(h == 0, dx_got, dx[:rows])]
    )

    own = []
    for g in range(2):
        e = ent_bg[g].reshape(2, N, -1).transpose(1, 0, 2).reshape(N, -1)
        own.append(jnp.concatenate([e, exp_bg[g].reshape(N, -1)], axis=1))
    own = own[0] + swap_h(own[1])
    six = jnp.stack(vec).reshape(6, N, T, sl).transpose(1, 2, 0, 3).reshape(N, T * 6 * sl)
    six = six + swap_c(six)
    six = six + swap_h(six)
    packed = jnp.concatenate([own, six], axis=1)
    for b in [1] + high_bits[::-1]:
        packed = packed + swap(packed, b, 0)
    packed = lax.dynamic_index_in_dim(packed, d, axis=0, keepdims=False)
    wide = own.shape[1]
    entry_bias_gradient = packed[: wide - eb].reshape(2, -1)
    expand_bias_gradient = packed[wide - eb : wide]
    six = packed[wide:].reshape(T, 6, sl)
    six = lax.dynamic_index_in_dim(six, t, axis=0, keepdims=False)
    return (
        layer_output,
        tokens_gradient,
        ent_grad.reshape(entry_weight.shape),
        entry_bias_gradient,
        mix_grad,
        six[5],
        six[3],
        six[4],
        exp_grad,
        expand_bias_gradient,
        nar_grad,
        six[2],
        six[0],
        six[1],
    )


def put_t(own, got, bit):
    on = bit == 1
    return jnp.concatenate([jnp.where(on, got, own), jnp.where(on, own, got)], axis=1)


def solution(mesh):
    body = functools.partial(local, mesh.shape["dp"], mesh.shape["tensor"])
    return jax.shard_map(
        body,
        mesh=mesh,
        in_specs=(
            P("dp", "tensor", None),
            P("dp", None),
            P("dp", None, "tensor"),
            P(None, ("tensor", "dp")),
            P("tensor", "dp"),
            P(("dp", "tensor")),
            P(("dp", "tensor")),
            P(("dp", "tensor")),
            P("dp", "tensor"),
            P(("tensor", "dp")),
            P("tensor", "dp"),
            P(("dp", "tensor")),
            P(("dp", "tensor")),
            P(("dp", "tensor")),
            P("dp", "tensor", None),
        ),
        out_specs=(
            P("dp", "tensor", None),
            P("dp", "tensor", None),
            P("dp", None, "tensor"),
            P(None, ("tensor", "dp")),
            P("tensor", "dp"),
            P(("dp", "tensor")),
            P(("dp", "tensor")),
            P(("dp", "tensor")),
            P("dp", "tensor"),
            P(("tensor", "dp")),
            P("tensor", "dp"),
            P(("dp", "tensor")),
            P(("dp", "tensor")),
            P(("dp", "tensor")),
        ),
        check_vma=False,
    )
```

```python
import functools
import jax
import jax.numpy as jnp
from jax import lax
from jax.experimental import pallas as pl
from jax.experimental.pallas import tpu as pltpu
from jax.sharding import PartitionSpec as P

HEAD = 64
BF = jnp.bfloat16
F32 = jnp.float32
FAR = 2.0**50


def nn(a, b):
    return lax.dot_general(a, b, (((1,), (0,)), ((), ())), preferred_element_type=F32)


def nt(a, b):
    return lax.dot_general(a, b, (((1,), (1,)), ((), ())), preferred_element_type=F32)


def tn(a, b):
    return lax.dot_general(a, b, (((0,), (0,)), ((), ())), preferred_element_type=F32)


def vspec():
    return pl.BlockSpec(memory_space=pltpu.VMEM)


def sspec():
    return pl.BlockSpec(memory_space=pltpu.SMEM)


def window(seg, first, size, step, total):
    low = seg[first]
    high = seg[first + size - 1]
    start = jnp.int32(0)
    stop = jnp.int32(total // step)
    for i in range(total // step):
        start = start + jnp.where(seg[i * step + step - 1] < low, 1, 0)
        stop = stop - jnp.where(seg[i * step] > high, 1, 0)
    return start, stop


def slot_block(s, h, c):
    return 2 * ((s % 2) ^ h) + ((s // 2) ^ c)


def by_window(seg, b, size, step, total, widths, body):
    start, stop = window(seg, b * size, size, step, total)
    before = 0
    for width in widths:
        count = stop - start
        hit = jnp.logical_and(count > before // step, count <= width // step)
        at = jnp.minimum(start, (total - width) // step) * step

        @pl.when(hit)
        def _(at=at, width=width):
            body(pl.multiple_of(at, step), width)

        before = width


def widths_of(rows):
    return (rows // 2, 3 * rows // 4, rows)


def fold(op, s):
    rows, lanes = s.shape
    return op(op(s.reshape(rows // 64, 64, lanes), axis=0), axis=0, keepdims=True)


def marks(seg_col):
    lane = lax.broadcasted_iota(jnp.int32, (seg_col.shape[0], 128), 1)
    same = seg_col == lane
    return (
        jnp.where(same, FAR, 0.0).astype(BF),
        jnp.where(same, 0.0, -FAR).astype(BF),
    )


def split_queries(pair, last):
    low = lax.broadcasted_iota(jnp.int32, pair.shape, 1) < HEAD
    zero = jnp.zeros_like(pair)
    return (
        jnp.where(low, pair, zero),
        jnp.where(low, zero, pair),
        jnp.where(low, zero, pltpu.roll(last, HEAD, 1)),
    )


def attend_forward_kernel(
    place, seg, x, w, bias, seg_col, qm, packed, context, out_t, logs, qmark, kmark
):
    rows = x.shape[0]
    size = rows // 4
    h, c = place[0], place[1]
    qmark[...], kmark[...] = marks(seg_col[...])

    for first, last in ((0, 256), (256, 512), (512, 576)):
        p = nn(x[...], w[:, first:last]) + bias[:, first:last]
        for s in range(4):
            at = pl.ds(pl.multiple_of(slot_block(s, h, c) * size, size), size)
            packed[at, first:last] = p[s * size : (s + 1) * size].astype(BF)

    def block(b, _):
        own = pl.ds(pl.multiple_of(b * size, size), size)
        scale = HEAD**-0.5
        q = split_queries(
            packed[own, 0:128].astype(F32) * scale, packed[own, 384:512].astype(F32) * scale
        )
        for i in range(3):
            qm[i, own, :] = q[i].astype(BF)

        def body(start, width):
            at = pl.ds(start, width)
            far = kmark[at, :]
            near = qmark[own, :]
            keys = (
                jnp.concatenate([packed[at, 128:256], far], axis=1),
                jnp.concatenate([packed[at, 384:512], far], axis=1),
            )
            v_pair = packed[at, 256:384].T
            v_t = (v_pair[:HEAD], v_pair[HEAD:], packed[at, 512:576].T)
            s = [
                nt(keys[i // 2], jnp.concatenate([qm[i, own, :], near], axis=1))
                for i in range(3)
            ]
            outs = []
            for i in range(3):
                top = fold(jnp.max, s[i])
                p = jnp.exp(s[i] - top)
                total = fold(jnp.sum, p)
                o = nn(v_t[i], p.astype(BF)) / total
                out_t[b, i * HEAD : (i + 1) * HEAD, :] = o
                logs[b, i : i + 1, :] = top + jnp.log(total)
                outs.append(o)
            context[own, 0:128] = jnp.concatenate(outs[:2], axis=0).T.astype(BF)
            context[own, 128:192] = outs[2].T.astype(BF)

        by_window(seg, b, size, size // 2, rows, widths_of(rows), body)
        return 0

    lax.fori_loop(0, 4, block, 0)


def attend_forward(place, seg, x, w, bias, seg_col):
    rows = x.shape[0]
    return pl.pallas_call(
        attend_forward_kernel,
        name="attend_forward",
        out_shape=(
            jax.ShapeDtypeStruct((3, rows, 128), BF),
            jax.ShapeDtypeStruct((rows, 576), BF),
            jax.ShapeDtypeStruct((rows, 192), BF),
            jax.ShapeDtypeStruct((4, 192, rows // 4), F32),
            jax.ShapeDtypeStruct((4, 8, rows // 4), F32),
        ),
        in_specs=[sspec(), sspec()] + [vspec()] * 4,
        out_specs=(vspec(),) * 5,
        scratch_shapes=[pltpu.VMEM((rows, 128), BF)] * 2,
    )(place, seg, x, w, bias, seg_col)


def attend_backward_kernel(
    place, seg, x, gf, wm, qm, packed, context, out_t, logs, seg_col,
    slots, grads, bias_grad,
    qmark, kmark, go, acc_k, acc_v, acc_l, acc_w, ctx_s,
):
    rows = x.shape[0]
    size = rows // 4
    h, c = place[0], place[1]
    qmark[...], kmark[...] = marks(seg_col[...])
    low = lax.broadcasted_iota(jnp.int32, (size, 128), 1) < HEAD
    for ref in (acc_k, acc_v, acc_l, acc_w):
        ref[...] = jnp.zeros_like(ref)
    p = nn(gf[...], wm[...]).astype(BF)
    for s in range(4):
        at = pl.ds(pl.multiple_of(slot_block(s, h, c) * size, size), size)
        go[at, :] = p[s * size : (s + 1) * size]
        ctx_s[s * size : (s + 1) * size, :] = context[at, :]

    def block(b, _):
        own = pl.ds(pl.multiple_of(b * size, size), size)
        slot = 2 * ((b % 2) ^ c) + ((b // 2) ^ h)
        mine = pl.ds(pl.multiple_of(slot * size, size), size)
        pair = go[own, 0:128]
        last = go[own, 128:192]
        zero = jnp.zeros_like(pair)
        g = (jnp.where(low, pair, zero), jnp.where(low, zero, pair), last)
        prod = pair.astype(F32).T * out_t[b, 0:128, :]
        prod_l = last.astype(F32).T * out_t[b, 128:192, :]
        inner = (
            jnp.sum(prod[:HEAD], axis=0, keepdims=True),
            jnp.sum(prod[HEAD:], axis=0, keepdims=True),
            jnp.sum(prod_l, axis=0, keepdims=True),
        )
        near = qmark[own, :]
        q = [qm[i, own, :] for i in range(3)]
        log = [logs[b, i : i + 1, :] for i in range(3)]

        def body(start, width):
            at = pl.ds(start, width)
            far = kmark[at, :]
            pairs = (packed[at, 128:256], packed[at, 384:512])
            keys = [jnp.concatenate([a, far], axis=1) for a in pairs]
            vals = (packed[at, 256:384], packed[at, 256:384], packed[at, 512:576])
            low_p, low_s = [], []
            for i in range(3):
                s = nt(keys[i // 2], jnp.concatenate([q[i], near], axis=1))
                e = jnp.exp(s - log[i])
                d = nt(vals[i], g[i])
                low_p.append(e.astype(BF))
                low_s.append((e * (d - inner[i])).astype(BF))
            acc_v[at, :] += nn(low_p[0], g[0]) + nn(low_p[1], g[1])
            acc_w[at, :] += nn(low_p[2], g[2])
            acc_k[at, :] += nn(low_s[0], q[0]) + nn(low_s[1], q[1])
            acc_l[at, :] += nn(low_s[2], q[2])
            k_t = pairs[0].T
            q_t = jnp.concatenate(
                [nn(k_t[:HEAD], low_s[0]), nn(k_t[HEAD:], low_s[1])], axis=0
            )
            l_t = nn(pairs[1].T, low_s[2])[HEAD:]
            slots[mine, 0:128] = (q_t.T * HEAD**-0.5).astype(BF)
            slots[mine, 384:448] = (l_t.T * HEAD**-0.5).astype(BF)

        by_window(seg, b, size, size // 2, rows, widths_of(rows), body)
        return 0

    lax.fori_loop(0, 4, block, 0)
    for s in range(4):
        at = pl.ds(pl.multiple_of(slot_block(s, h, c) * size, size), size)
        to = slice(s * size, (s + 1) * size)
        slots[to, 128:256] = acc_k[at, :].astype(BF)
        slots[to, 256:384] = acc_v[at, :].astype(BF)
        slots[to, 448:512] = acc_l[at, HEAD:].astype(BF)
        slots[to, 512:576] = acc_w[at, :].astype(BF)
    bias_grad[0:1, :] = jnp.sum(slots[...].astype(F32), axis=0, keepdims=True)
    grads[:, 0:576] = tn(x[...], slots[...]).astype(BF)
    grads[:, 576:768] = tn(gf[...], ctx_s[...]).astype(BF)


def attend_backward(place, seg, x, gf, wm, qm, packed, context, out_t, logs, seg_col):
    rows, features = x.shape
    return pl.pallas_call(
        attend_backward_kernel,
        name="attend_backward",
        out_shape=(
            jax.ShapeDtypeStruct((rows, 576), BF),
            jax.ShapeDtypeStruct((features, 768), BF),
            jax.ShapeDtypeStruct((8, 576), F32),
        ),
        in_specs=[sspec(), sspec()] + [vspec()] * 9,
        out_specs=(vspec(),) * 3,
        scratch_shapes=[
            pltpu.VMEM((rows, 128), BF),
            pltpu.VMEM((rows, 128), BF),
            pltpu.VMEM((rows, 192), BF),
            pltpu.VMEM((rows, 128), F32),
            pltpu.VMEM((rows, 128), F32),
            pltpu.VMEM((rows, 128), F32),
            pltpu.VMEM((rows, HEAD), F32),
            pltpu.VMEM((rows, 192), BF),
        ],
    )(place, seg, x, gf, wm, qm, packed, context, out_t, logs, seg_col)


def mix_kernel(place, a, b, wa, wb, out):
    out[...] = (nt(a[...], wa[...]) + nt(b[...], wb[...])).astype(BF)


def mix(place, a, b, wa, wb):
    rows, width = a.shape
    features = wa.shape[0]
    size = rows // 4
    nat = pl.BlockSpec((size, width), lambda s, p: (slot_block(s, p[0], p[1]), 0))
    full = pl.BlockSpec((features, width), lambda s, p: (0, 0))
    return pl.pallas_call(
        mix_kernel,
        name="mix",
        out_shape=jax.ShapeDtypeStruct((rows, features), BF),
        grid_spec=pltpu.PrefetchScalarGridSpec(
            num_scalar_prefetch=1,
            grid=(4,),
            in_specs=[nat, nat, full, full],
            out_specs=pl.BlockSpec((size, features), lambda s, p: (s, 0)),
        ),
    )(place, a, b, wa, wb)


def mean_last(v):
    return jnp.mean(v, axis=-1, keepdims=True)


def normalize(v):
    center = v - mean_last(v)
    scale = lax.rsqrt(mean_last(center * center) + 1e-12)
    return center * scale, scale


def norm_backward(grad, hat, scale, gain):
    e = grad * gain
    return scale * (e - mean_last(e) - hat * mean_last(e * hat))


def rows_spec(size, lanes):
    return pl.BlockSpec((size, lanes), lambda s: (s, 0))


def other_spec(size, lanes):
    return pl.BlockSpec((size, lanes), lambda s: (s ^ 2, 0))


def whole(shape):
    return pl.BlockSpec(shape, lambda s: (0,) * len(shape))


def spread(pieces):
    out = []
    at = 0
    for p in pieces:
        out.append((p, at, at + p.shape[1]))
        at += p.shape[1]
    return out


def ffn_forward_kernel(count, x, mine, got, six, be, *refs):
    we, wn = refs[:count], refs[count : 2 * count]
    hat, scale, low, act, slope, branch = refs[2 * count :]
    v = x[...].astype(F32) + (mine[...].astype(F32) + got[...].astype(F32)) + six[0:1, :]
    unit, r = normalize(v)
    hat[...] = unit
    scale[...] = r
    n = (unit * six[1:2, :] + six[2:3, :]).astype(BF)
    low[...] = n
    for w, a, b in spread(we):
        inner = nn(n, w[...]) + be[:, a:b]
        cdf = 0.5 * (1.0 + lax.erf(inner * 0.7071067811865476))
        act[:, a:b] = (inner * cdf).astype(BF)
        slope[:, a:b] = (
            cdf + inner * jnp.exp(-0.5 * inner * inner) * 0.3989422804014327
        ).astype(BF)
    total = None
    for w, a, b in spread(wn):
        part = nt(act[:, a:b], w[...])
        total = part if total is None else total + part
    branch[...] = total.astype(BF)


def ffn_forward(x, mine, got, six, be, we, wn):
    rows, features = x.shape
    units = be.shape[1]
    size = rows // 4
    return pl.pallas_call(
        functools.partial(ffn_forward_kernel, len(we)),
        name="ffn_forward",
        grid=(4,),
        out_shape=(
            jax.ShapeDtypeStruct((rows, features), F32),
            jax.ShapeDtypeStruct((rows, 1), F32),
            jax.ShapeDtypeStruct((rows, features), BF),
            jax.ShapeDtypeStruct((rows, units), BF),
            jax.ShapeDtypeStruct((rows, units), BF),
            jax.ShapeDtypeStruct((rows, features), BF),
        ),
        in_specs=[
            rows_spec(size, features),
            rows_spec(size, features),
            other_spec(size, features),
            whole((8, features)),
            whole((1, units)),
        ]
        + [whole(w.shape) for w in (*we, *wn)],
        out_specs=(
            rows_spec(size, features),
            rows_spec(size, 1),
            rows_spec(size, features),
            rows_spec(size, units),
            rows_spec(size, units),
            rows_spec(size, features),
        ),
    )(x, mine, got, six, be, *we, *wn)


def ffn_backward_kernel(count, hat, mine, got, six, cot, slope, *refs):
    we, wn = refs[:count], refs[count : 2 * count]
    out, grad2, gs, gi, dn, vec, bias = refs[2 * count :]
    s = pl.program_id(0)
    normed = hat[...] * six[1:2, :] + six[2:3, :]
    v = normed + (mine[...].astype(F32) + got[...].astype(F32)) + six[3:4, :]
    unit, r = normalize(v)
    g = cot[...].astype(F32)
    grad = norm_backward(g, unit, r, six[4:5, :])
    grad2[...] = grad
    low = grad.astype(BF)
    gs[...] = low

    @pl.when(s == 0)
    def _():
        vec[...] = jnp.zeros_like(vec)
        bias[...] = jnp.zeros_like(bias)

    @pl.when(s < 2)
    def _():
        out[...] = (unit * six[4:5, :] + six[5:6, :]).astype(BF)
        vec[0:1, :] += jnp.sum(g * unit, axis=0, keepdims=True)
        vec[1:2, :] += jnp.sum(g, axis=0, keepdims=True)
        vec[2:3, :] += jnp.sum(grad, axis=0, keepdims=True)

    for w, a, b in spread(wn):
        d = (nn(low, w[...]) * slope[:, a:b].astype(F32)).astype(BF)
        gi[:, a:b] = d
        bias[0:1, a:b] += jnp.sum(d.astype(F32), axis=0, keepdims=True)
    total = None
    for w, a, b in spread(we):
        part = nt(gi[:, a:b], w[...])
        total = part if total is None else total + part
    dn[...] = total.astype(BF)


def ffn_backward(hat, mine, got, six, cot, slope, we, wn):
    rows, features = hat.shape
    units = slope.shape[1]
    size = rows // 4
    return pl.pallas_call(
        functools.partial(ffn_backward_kernel, len(we)),
        name="ffn_backward",
        grid=(4,),
        out_shape=(
            jax.ShapeDtypeStruct((rows // 2, features), BF),
            jax.ShapeDtypeStruct((rows, features), F32),
            jax.ShapeDtypeStruct((rows, features), BF),
            jax.ShapeDtypeStruct((rows, units), BF),
            jax.ShapeDtypeStruct((rows, features), BF),
            jax.ShapeDtypeStruct((8, features), F32),
            jax.ShapeDtypeStruct((8, units), F32),
        ),
        in_specs=[
            rows_spec(size, features),
            rows_spec(size, features),
            other_spec(size, features),
            whole((8, features)),
            rows_spec(size, features),
            rows_spec(size, units),
        ]
        + [whole(w.shape) for w in (*we, *wn)],
        out_specs=(
            pl.BlockSpec((size, features), lambda s: (jnp.minimum(s, 1), 0)),
            rows_spec(size, features),
            rows_spec(size, features),
            rows_spec(size, units),
            rows_spec(size, features),
            whole((8, features)),
            whole((8, units)),
        ),
    )(hat, mine, got, six, cot, slope, *we, *wn)


def weight_grad_kernel(cut, a, b, first, second, both):
    units = b.shape[1] // 2
    p = tn(a[...], b[...]).astype(BF)
    first[...] = p[:, :cut]
    second[...] = p[:, units : units + cut]
    both[:, : units - cut] = p[:, cut:units]
    both[:, units - cut :] = p[:, units + cut :]


def weight_grad(a, b, cut):
    rows, features = a.shape
    units = b.shape[1] // 2
    size = 256
    widths = (cut, cut, 2 * (units - cut))
    return pl.pallas_call(
        functools.partial(weight_grad_kernel, cut),
        name="weight_grad",
        grid=(features // size,),
        out_shape=tuple(jax.ShapeDtypeStruct((features, n), BF) for n in widths),
        in_specs=[
            pl.BlockSpec((rows, size), lambda m: (0, m)),
            whole((rows, 2 * units)),
        ],
        out_specs=tuple(rows_spec(size, n) for n in widths),
    )(a, b)


def first_norm_kernel(grad2, mine, got, hat, scale, six, gf, own, vec):
    s = pl.program_id(0)
    g = grad2[...] + (mine[...].astype(F32) + got[...].astype(F32))
    grad = norm_backward(g, hat[...], scale[...], six[1:2, :])
    gf[...] = grad.astype(BF)

    @pl.when(s == 0)
    def _():
        vec[...] = jnp.zeros_like(vec)

    @pl.when(s < 2)
    def _():
        own[...] = grad
        vec[0:1, :] += jnp.sum(g * hat[...], axis=0, keepdims=True)
        vec[1:2, :] += jnp.sum(g, axis=0, keepdims=True)
        vec[2:3, :] += jnp.sum(grad, axis=0, keepdims=True)


def first_norm(grad2, mine, got, hat, scale, six):
    rows, features = hat.shape
    size = rows // 4
    return pl.pallas_call(
        first_norm_kernel,
        name="first_norm",
        grid=(4,),
        out_shape=(
            jax.ShapeDtypeStruct((rows, features), BF),
            jax.ShapeDtypeStruct((rows // 2, features), F32),
            jax.ShapeDtypeStruct((8, features), F32),
        ),
        in_specs=[
            rows_spec(size, features),
            rows_spec(size, features),
            other_spec(size, features),
            rows_spec(size, features),
            rows_spec(size, 1),
            whole((8, features)),
        ],
        out_specs=(
            rows_spec(size, features),
            pl.BlockSpec((size, features), lambda s: (jnp.minimum(s, 1), 0)),
            whole((8, features)),
        ),
    )(grad2, mine, got, hat, scale, six)


def tokens_grad_kernel(a, b, wa, wb, base, other, own):
    j = pl.program_id(0)
    p = nt(a[...], wa[...]) + nt(b[...], wb[...])

    @pl.when(j < 2)
    def _():
        other[...] = p.astype(BF)

    @pl.when(j >= 2)
    def _():
        own[...] = p + base[...]


def tokens_grad(a, b, wa, wb, base):
    rows, width = a.shape
    features = wa.shape[0]
    size = rows // 4
    turned = pl.BlockSpec((size, width), lambda j: (j ^ 2, 0))
    early = pl.BlockSpec((size, features), lambda j: (jnp.minimum(j, 1), 0))
    late = pl.BlockSpec((size, features), lambda j: (jnp.maximum(j - 2, 0), 0))
    return pl.pallas_call(
        tokens_grad_kernel,
        name="tokens_grad",
        grid=(4,),
        out_shape=(
            jax.ShapeDtypeStruct((rows // 2, features), BF),
            jax.ShapeDtypeStruct((rows // 2, features), F32),
        ),
        in_specs=[turned, turned, whole((features, width)), whole((features, width)), late],
        out_specs=(early, late),
    )(a, b, wa, wb, base)


def after(x, deps):
    return lax.optimization_barrier((x, deps))[0] if deps else x


class Order:
    def __init__(self, dp_size, tensor_size):
        self.n, self.t = dp_size, tensor_size
        self.sent = []

    def swap(self, x, dp_bit, t_bit, deps=()):
        x = after(x, [*deps, *self.sent])
        self.sent = [x]
        pairs = [
            (i * self.t + j, (i ^ dp_bit) * self.t + (j ^ t_bit))
            for i in range(self.n)
            for j in range(self.t)
        ]
        return lax.ppermute(x, ("dp", "tensor"), pairs)


class Chain:
    def __init__(self, order, steps, deps=()):
        self.order, self.steps, self.done = order, steps, False
        self.run(None, deps)

    def run(self, got, deps):
        try:
            x, dp_bit, t_bit = self.steps.send(got)
            self.got = self.order.swap(x, dp_bit, t_bit, deps)
        except StopIteration as end:
            self.done, self.result = True, end.value

    def go(self, *deps):
        if not self.done:
            self.run(after(self.got, list(deps)), deps)
        return self

    def all(self, *deps):
        while not self.done:
            self.go(*deps)
        return self.result


def pack(q, k, v):
    return jnp.concatenate(
        [a[..., :128] for a in (q, k, v)] + [a[..., 128:] for a in (q, k, v)], axis=-1
    )


def unpack(a):
    return tuple(
        jnp.concatenate(
            [a[..., 128 * i : 128 * i + 128], a[..., 384 + 64 * i : 448 + 64 * i]], axis=-1
        )
        for i in range(3)
    )


def local(
    dp_size,
    tensor_size,
    tokens,
    segment_ids,
    entry_weight,
    entry_bias,
    mixing_weight,
    mixing_bias,
    first_gain,
    first_shift,
    expand_weight,
    expand_bias,
    narrowing_matrix,
    reduce_bias,
    second_gain,
    second_shift,
    layer_cotangent,
):
    N, T = dp_size, tensor_size
    d = lax.axis_index("dp")
    t = lax.axis_index("tensor")
    h = t // 2
    c = t % 2
    D = tokens.shape[-1]
    order = Order(N, T)
    chain = functools.partial(Chain, order)
    high = []
    bit = N // 2
    while bit >= 2:
        high.append(bit)
        bit //= 2
    H = (0, 2)
    Y = (1, 0)

    def is_on(b):
        return (d // b) % 2 == 1

    def flat(a):
        return a.reshape(-1, a.shape[-1])

    def place(a, got, b):
        blocks, rows, lanes = a.shape
        on = is_on(b)
        both = jnp.stack([jnp.where(on, got, a), jnp.where(on, a, got)], axis=1)
        return both.reshape(2 * blocks, rows, lanes)

    def gather_high(a):
        a = a[None]
        for b in high:
            a = place(a, (yield a, b, 0), b)
        return a

    def gather_yx(a):
        a = place(a, (yield (a, *Y)), 1)
        return flat(a), flat((yield (a, *H)))

    def gather_xy(a):
        lanes = a.shape[2]
        both = jnp.concatenate([a, (yield (a, *H))], axis=2)
        both = place(both, (yield (both, *Y)), 1)
        return flat(both[:, :, :lanes]), flat(both[:, :, lanes:])

    def add(a, b, low=True):
        s = a.astype(F32) + b.astype(F32)
        return s.astype(BF) if low else s

    def halves(a, b):
        n, r, lanes = a.shape
        a = a.reshape(n // 2, 2, r, lanes)
        on = is_on(b)
        return jnp.where(on, a[:, 1], a[:, 0]), jnp.where(on, a[:, 0], a[:, 1])

    def blocks(a):
        return a.reshape(N, D // N, -1)

    def scatter_xy(first, second):
        a = add(blocks(first), (yield (blocks(second), *H)))
        keep, send = halves(a, 1)
        return add(keep, (yield (send, *Y)))

    def scatter_yx(both):
        keep, send = halves(blocks(both), 1)
        b = add(keep, (yield (send, *Y)))
        half = b.shape[2] // 2
        return add(b[:, :, :half], (yield (b[:, :, half:], *H)))

    def scatter_high(a, low):
        bits = high[::-1]
        for i, b in enumerate(bits):
            keep, send = halves(a, b)
            a = add(keep, (yield send, b, 0), low or i + 1 < len(bits))
        return a.reshape(D // N, -1)

    def scatter_late(a):
        keep, send = halves(blocks(a), 1)
        a = add(keep, (yield (send, *Y)))
        return (yield from scatter_high(a, True))

    sl = first_gain.shape[0]
    eb = expand_bias.shape[0]
    bb = entry_bias.shape[1]
    small = jnp.concatenate(
        [
            mixing_bias,
            first_gain,
            first_shift,
            reduce_bias,
            second_gain,
            second_shift,
            entry_bias.astype(F32).reshape(-1),
            expand_bias.astype(F32),
        ]
    )
    small = jnp.pad(small, (0, -small.shape[0] % 128)).reshape(1, 1, -1)

    def gather_small(a):
        def put(own, got, on):
            return jnp.concatenate(
                [jnp.where(on, got, own), jnp.where(on, own, got)], axis=1
            )

        a = put(a, (yield a, 0, 1), c == 1)
        a = put(a, (yield (a, *H)), h == 1)
        for b in high + [1]:
            a = place(a, (yield a, b, 0), b)
        return a

    def pick(a):
        return jnp.where(h == 0, a[0], a[1]), jnp.where(h == 0, a[1], a[0])

    def to_chip(a):
        keep, send = pick(a)
        own = jnp.concatenate([keep, (yield (send, *H))], axis=0)
        return jnp.concatenate([own, (yield own, 0, 1)], axis=0)

    def from_chip(own, got):
        return jnp.stack([jnp.where(h == 0, own, got), jnp.where(h == 0, got, own)])

    units = expand_weight.shape[1]
    cut = 256
    entry = chain(gather_high(pack(*(entry_weight[:, i] for i in range(3)))))
    x = chain(to_chip(tokens))
    smalls = chain(gather_small(small))
    entry.go()
    smalls.go()
    expand = chain(
        gather_high(jnp.concatenate([expand_weight, mixing_weight.T], axis=1))
    )
    e = entry.all()
    smalls.go()
    entry_a = chain(gather_yx(e[:, :, :256]))
    entry_b = chain(gather_xy(e[:, :, 256:]))
    narrow = chain(gather_high(narrowing_matrix.T))
    x.go()
    smalls.go()
    expand.go()
    entry_a.go()
    entry_b.go()
    narrow.go()
    smalls.go()
    f = expand.all()
    mixing = chain(gather_xy(f[:, :, units:]))
    expand_a = chain(gather_yx(f[:, :, :cut]))
    expand_b = chain(gather_xy(f[:, :, cut:units]))
    x = x.all()
    a, b = entry_a.all(), entry_b.all()
    wq = [jnp.concatenate([a[g], b[g]], axis=1) for g in range(2)]
    small = smalls.all()

    six = small[:, :, : 6 * sl].reshape(N, T, 6, sl).transpose(2, 0, 1, 3).reshape(6, D)
    six = jnp.pad(six, ((0, 2), (0, 0)))
    q_bias, e_bias = [], []
    for index in (t, t ^ 2):
        m = lax.dynamic_index_in_dim(small, index, axis=1, keepdims=False)
        e = m[:, 6 * sl : 6 * sl + 2 * bb].reshape(N, 2, bb)
        e = e.transpose(1, 0, 2).reshape(2, 1, -1)
        q_bias.append(pack(e[0], jnp.zeros_like(e[0]), e[1]))
        e_bias.append(m[:, 6 * sl + 2 * bb : 6 * sl + 2 * bb + eb].reshape(1, -1))
    e_bias = jnp.concatenate(e_bias, axis=1)

    seg = jnp.where(h == 0, segment_ids[0], segment_ids[1])
    seg_col = seg.reshape(-1, 1)
    place_hc = jnp.stack([h, c]).astype(jnp.int32)

    state = []
    state.append(
        attend_forward(place_hc, seg, after(x, order.sent), wq[0], q_bias[0], seg_col)
    )
    end = state[0][2]
    mixing.go(end)
    expand_a.go(end)
    expand_b.go(end)
    n = narrow.all(end)
    narrow_a = chain(gather_yx(n[:, :, :cut]), (end,))
    narrow_b = chain(gather_xy(n[:, :, cut:]), (end,))
    state.append(
        attend_forward(
            place_hc, seg, after(x, [*order.sent, end]), wq[1], q_bias[1], seg_col
        )
    )
    end = state[1][2]
    wm = mixing.all(end)
    mixed = mix(place_hc, state[0][2], end, wm[0], wm[1])
    mixed_got = order.swap(mixed, 0, 1)
    cot = chain(to_chip(layer_cotangent), (mixed,))
    ea, eb_ = expand_a.all(mixed), expand_b.all(mixed)
    we = (ea[0], eb_[0], ea[1], eb_[1])
    narrow_a.go(mixed)
    narrow_b.go(mixed)
    na, nb = narrow_a.all(mixed), narrow_b.all(mixed)
    wn = (na[0], nb[0], na[1], nb[1])
    cot.go(mixed)
    hat, scale, low, act, slope, branch = ffn_forward(
        x, mixed, mixed_got, six, e_bias, we, wn
    )
    branch_got = order.swap(branch, 0, 1)
    cot = cot.all(branch)

    out, grad2, gs, gi, dn, vec2, exp_bias = ffn_backward(
        hat, branch, branch_got, six, cot, slope, we, wn
    )
    rows = tokens.shape[1]
    dn_got = order.swap(dn, 0, 1)
    first, second, both = weight_grad(after(gs, order.sent), act, cut)
    nar_a = chain(scatter_xy(first, second))
    nar_b = chain(scatter_yx(both))
    first, second, both = weight_grad(after(low, order.sent), gi, cut)
    exp_a = chain(scatter_xy(first, second))
    exp_b = chain(scatter_yx(both))
    gf, grad1, vec1 = first_norm(
        after(grad2, order.sent), dn, dn_got, hat, scale, six
    )
    out_got = order.swap(out[rows:], *H, (gf,))
    layer_output = from_chip(out[:rows], out_got)
    nar_a.go(gf)
    nar_b.go(gf)
    results = [None, None]
    late = [None, None]

    def backward(g):
        qm, packed, context, out_t, logs = state[g]
        return attend_backward(
            place_hc, seg, x, after(gf, order.sent), wm[g], qm, packed, context, out_t,
            logs, seg_col,
        )

    results[1] = backward(1)
    end = results[1][1]
    nar = chain(
        scatter_high(jnp.concatenate([nar_a.all(end), nar_b.all(end)], axis=2), False),
        (end,),
    )
    late[1] = chain(scatter_late(end), (end,))
    exp_a.go(end)
    exp_b.go(end)
    results[0] = backward(0)
    end = results[0][1]
    late[0] = chain(scatter_late(end), (end,))
    late[1].go(end)
    nar.go(end)
    exp = chain(
        scatter_high(jnp.concatenate([exp_a.all(end), exp_b.all(end)], axis=2), False),
        (end,),
    )
    dx_other, dx_own = tokens_grad(
        after(results[0][0], order.sent), results[1][0], wq[0], wq[1], grad1
    )
    dx_got = order.swap(dx_other, 0, 1)
    late[1].go(dx_other)
    late[0].go(dx_other)
    exp.go(dx_other)
    nar.go(dx_other)
    dx = dx_own + dx_got.astype(F32)
    dx_got = order.swap(dx[rows:].astype(BF), *H).astype(F32)
    tokens_gradient = from_chip(dx[:rows], dx_got)

    own = []
    for g in range(2):
        e = unpack(results[g][2][0])
        e = jnp.stack([e[0], e[2]]).reshape(2, N, bb).transpose(1, 0, 2).reshape(N, 2 * bb)
        f = exp_bias[0, g * units : (g + 1) * units].reshape(N, eb)
        own.append(jnp.concatenate([e, f], axis=1))
    six = jnp.concatenate([vec1[:3], vec2[:3]])
    six = six.reshape(6, N, T, sl).transpose(1, 2, 0, 3).reshape(N, T * 6 * sl)

    def sum_small(own, other, six):
        six = six + (yield six, 0, 1)
        wide = own.shape[1]
        got = yield (jnp.concatenate([other, six], axis=1), *H)
        a = jnp.concatenate([own, six], axis=1) + got
        for b in [1] + high[::-1]:
            a = a + (yield a, b, 0)
        return a

    small = chain(sum_small(own[0], own[1], six))
    while not (late[0].done and late[1].done and small.done):
        late[1].go()
        late[0].go()
        small.go()
    late_got = order.swap(late[1].result, *H)
    late = add(late[0].result, late_got, False)
    nar_grad = nar.all().T
    exp_grad = exp.all()
    ent_grad = jnp.stack(unpack(late[:, :576]), axis=1)
    mix_grad = late[:, 576:].T
    packed = lax.dynamic_index_in_dim(small.result, d, axis=0, keepdims=False)
    entry_bias_gradient = packed[: 2 * bb].reshape(2, bb)
    expand_bias_gradient = packed[2 * bb : 2 * bb + eb]
    six = packed[2 * bb + eb :].reshape(T, 6, sl)
    six = lax.dynamic_index_in_dim(six, t, axis=0, keepdims=False)
    return (
        layer_output,
        tokens_gradient,
        ent_grad,
        entry_bias_gradient,
        mix_grad,
        six[2],
        six[0],
        six[1],
        exp_grad,
        expand_bias_gradient,
        nar_grad,
        six[5],
        six[3],
        six[4],
    )


def solution(mesh):
    body = functools.partial(local, mesh.shape["dp"], mesh.shape["tensor"])
    return jax.shard_map(
        body,
        mesh=mesh,
        in_specs=(
            P("dp", "tensor", None),
            P("dp", None),
            P("dp", None, "tensor"),
            P(None, ("tensor", "dp")),
            P("tensor", "dp"),
            P(("dp", "tensor")),
            P(("dp", "tensor")),
            P(("dp", "tensor")),
            P("dp", "tensor"),
            P(("tensor", "dp")),
            P("tensor", "dp"),
            P(("dp", "tensor")),
            P(("dp", "tensor")),
            P(("dp", "tensor")),
            P("dp", "tensor", None),
        ),
        out_specs=(
            P("dp", "tensor", None),
            P("dp", "tensor", None),
            P("dp", None, "tensor"),
            P(None, ("tensor", "dp")),
            P("tensor", "dp"),
            P(("dp", "tensor")),
            P(("dp", "tensor")),
            P(("dp", "tensor")),
            P("dp", "tensor"),
            P(("tensor", "dp")),
            P("tensor", "dp"),
            P(("dp", "tensor")),
            P(("dp", "tensor")),
            P(("dp", "tensor")),
        ),
        check_vma=False,
    )
```
